32 devices in a mesh: dev: 32 (over z, y, x, core).
Axes of the slice: x: 2, y: 2, z: 4, core: 2. Of those that a mesh axis runs over, the one named last changes fastest.
Arguments:
- images: bfloat16 [256, 768, 1536], P('dev'), may hold values from -6 to 6
- legendre: bfloat16 [32, 704, 768], P('dev'), may hold values from -0.21875 to 0.21875
- leakage: float32 [32, 3, 13, 704], P('dev'), may hold values from -1 to 1
Outputs:
- modes: float32 [32, 704, 512], P('dev')
The draws below stay inside these ranges and needn't reach their ends.
All inputs are finite; a program needn't handle non-finite values.
Results may differ from the reference program's by a relative error of at most 0.0053.
Values may be sent and summed in bfloat16 or wider, within the bound.
A program may use at most 128 MiB of HBM per device.

```python
import math
import jax
import jax.numpy as jnp
from jax import lax

NLAT = 768
NLON = 1536
DEG = 704
BAND = 6
NT = 256
M_ORD = 32


def shard_levels(rng, extent, cuts, least, top_value):
    level = 1.0
    for axis_at, shards_of in cuts:
        draws = jax.random.uniform(jax.random.fold_in(jax.random.fold_in(rng, 6), axis_at), (shards_of,), jnp.float32, least / len(cuts), top_value / len(cuts))
        level = level * jnp.repeat(jnp.exp(draws), extent[axis_at] // shards_of).reshape((-1,) + (1,) * (len(extent) - 1 - axis_at))
    return level


def centred(rng, extent, deviation, limit, pieces=(), kind=jnp.bfloat16):
    entries = deviation * jax.random.normal(rng, extent, jnp.float32)
    if pieces:
        entries = entries * shard_levels(rng, extent, pieces, -0.22, 0.18)
    return jnp.clip(entries, -limit, limit).astype(kind)


def setup_inputs(seed: int = 0) -> dict:
    key_list = jax.random.split(jax.random.key(seed), 4)
    return {
        "images": centred(key_list[0], (NT, NLAT, NLON), 1.0, 6.0, ((0, 32),)),
        "legendre": centred(key_list[1], (M_ORD, DEG, NLAT), NLAT ** -0.5, 0.21875, ((0, 32),)),
        "leakage": centred(key_list[2], (M_ORD, 3, 2 * BAND + 1, DEG), 0.16, 1.0, ((0, 32),), jnp.float32),
    }


def lon_table(nlon, norders):
    index = jnp.arange(nlon, dtype=jnp.int32)[None, :]
    order = jnp.arange(norders, dtype=jnp.int32)[:, None]
    phase = (index * order % nlon).astype(jnp.float32)
    angle = 2.0 * math.pi * phase / nlon
    table = jnp.stack([jnp.cos(angle), -jnp.sin(angle)], axis=1) / math.sqrt(nlon)
    return table.reshape(2 * norders, nlon).astype(jnp.bfloat16)

def time_table(ntimes):
    index = jnp.arange(ntimes, dtype=jnp.int32)
    phase = (index[:, None] * index[None, :] % ntimes).astype(jnp.float32)
    angle = 2.0 * math.pi * phase / ntimes
    cosine = jnp.cos(angle)
    sine = jnp.sin(angle)
    upper = jnp.concatenate([cosine, -sine], axis=1)
    lower = jnp.concatenate([sine, cosine], axis=1)
    return (jnp.concatenate([upper, lower], axis=0) / math.sqrt(ntimes)).astype(jnp.bfloat16)

def reference(images, legendre, leakage):
    table = lon_table(NLON, M_ORD).astype(jnp.float32)

    def one_image(image):
        out = jnp.dot(table, image.astype(jnp.float32).T, preferred_element_type=jnp.float32)
        return out.astype(jnp.bfloat16)
    lon = lax.map(one_image, images)
    lon = jnp.transpose(lon.reshape(NT, M_ORD, 2, NLAT), (1, 2, 0, 3))
    wtable = time_table(NT)
    degrees = jnp.arange(DEG, dtype=jnp.int32)

    def one_order(args):
        order, table_rows, data = args
        flat = data.reshape(2 * NT, NLAT)
        coef = lax.dot_general(table_rows, flat, (((1,), (1,)), ((), ())), preferred_element_type=jnp.float32)
        coef = jnp.where((degrees >= order)[:, None], coef, jnp.float32(0.0)).astype(jnp.bfloat16)
        return jnp.dot(coef, wtable, preferred_element_type=jnp.float32)
    orders = jnp.arange(M_ORD, dtype=jnp.int32)
    spectra = lax.map(one_order, (orders, legendre, lon))
    padded = jnp.pad(spectra, ((1, 1), (BAND, BAND), (0, 0)))

    def one_mode(args):
        order, coeffs = args
        rows = lax.dynamic_slice(padded, (order.astype(jnp.int32), jnp.int32(0), jnp.int32(0)), (3, DEG + 2 * BAND, 2 * NT))
        total = jnp.zeros((DEG, 2 * NT), jnp.float32)
        for shift in range(3):
            for offset in range(2 * BAND + 1):
                total = total + coeffs[shift, offset][:, None] * rows[shift, offset:offset + DEG]
        return jnp.where((degrees >= order)[:, None], total, jnp.float32(0.0))
    return lax.map(one_mode, (orders, leakage))
```

```python
import functools
import math

import jax
import jax.numpy as jnp
import numpy as np
from jax import lax
from jax.experimental import pallas as pl
from jax.experimental.pallas import tpu as pltpu
from jax.sharding import PartitionSpec as P

MESH = pl.DeviceIdType.MESH
BAND = 6
PAD = 16
F32 = jnp.float32
BF16 = jnp.bfloat16


def lon_table(nlon, norders):
    phase = (np.arange(nlon)[None, :] * np.arange(norders)[:, None]) % nlon
    angle = 2.0 * math.pi * phase / nlon
    table = np.stack([np.cos(angle), -np.sin(angle)], axis=1) / math.sqrt(nlon)
    return table.reshape(2 * norders, nlon).astype(np.float32).astype(BF16)


def time_table(ntimes, devices):
    phase = (np.arange(ntimes)[:, None] * np.arange(ntimes)[None, :]) % ntimes
    angle = 2.0 * math.pi * phase / ntimes
    cosine, sine = np.cos(angle), np.sin(angle)
    upper = np.concatenate([cosine, -sine], axis=1)
    lower = np.concatenate([sine, cosine], axis=1)
    table = np.concatenate([upper, lower], axis=0) / math.sqrt(ntimes)
    table = table.reshape(2, devices, ntimes // devices, 2 * ntimes).transpose(1, 0, 2, 3)
    return table.reshape(2 * ntimes, 2 * ntimes).astype(np.float32).astype(BF16)


def split(value):
    high = value.astype(BF16)
    low = (value - high.astype(F32)).astype(BF16)
    return high, low


def kernel(n, lat, nblk,
           images, legendre, leakage, table, wtable, out,
           img, tab, leg, leak, wt, scr, send, recv, coef, comb, bands, lk, lkt,
           img_sem, in_sem, a_send, a_recv, c_send, c_recv, out_sem):
    me = lax.axis_index("dev")
    t_local, nlat, nlon = images.shape
    rows = 2 * t_local
    nchunk = nlat // lat
    ktab = table.shape[0]
    degrees = legendre.shape[1]
    blk = degrees // nblk
    win = blk + 2 * PAD
    half = wtable.shape[0]

    def load(index, src, dst):
        return pltpu.make_async_copy(src, dst, in_sem.at[index])

    def image_copy(c, t):
        part = pl.ds(c * lat, lat)
        return pltpu.make_async_copy(images.at[t, part, :], img.at[t, part, :], img_sem.at[c, t])

    loads = [
        load(0, table, tab), load(1, legendre.at[0], leg), load(2, leakage.at[0], leak),
        load(3, wtable, wt),
    ]
    loads[0].start()
    for c in range(nchunk):
        for t in range(t_local):
            image_copy(c, t).start()
    for copy in loads[1:]:
        copy.start()

    barrier = pltpu.get_barrier_semaphore()

    def greet(o, carry):
        pl.semaphore_signal(barrier, inc=1, device_id=(lax.rem(me + o, n),), device_id_type=MESH)
        return carry

    lax.fori_loop(1, n, greet, 0)
    loads[0].wait()

    def lon_chunk(c, carry):
        for t in range(t_local):
            image_copy(c, t).wait()
            block = img[t, pl.ds(pl.multiple_of(c * lat, lat), lat), :]
            part = lax.dot_general(tab[...], block, (((1,), (1,)), ((), ())), preferred_element_type=F32)
            for j in range(lat // 128):
                scr[j, pl.ds(t, ktab, stride=t_local), :] = part[:, j * 128:(j + 1) * 128]
        for j in range(lat // 128):
            send[c, :, j * 128:(j + 1) * 128] = scr[j].astype(BF16)

        @pl.when(c == 0)
        def _():
            pl.semaphore_wait(barrier, n - 1)

        mine = pl.ds(pl.multiple_of(me * rows, rows), rows)

        def post(o, inner):
            to = lax.rem(me + o, n)
            theirs = pl.ds(pl.multiple_of(to * rows, rows), rows)
            pltpu.make_async_remote_copy(
                src_ref=send.at[c, theirs, :], dst_ref=recv.at[c, mine, :],
                send_sem=a_send.at[c], recv_sem=a_recv.at[c],
                device_id=(to,), device_id_type=MESH,
            ).start()
            return inner

        lax.fori_loop(1, n, post, 0)
        recv[c, mine, :] = send[c, mine, :]
        return carry

    lax.fori_loop(0, nchunk, lon_chunk, 0)

    loads[2].wait()
    lk[...] = jnp.zeros_like(lk)
    for d in range(3):
        lk[16 * d:16 * d + 2 * BAND + 1, 0:degrees] = leak[d]
    for j in range(lk.shape[1] // 128):
        lkt[j * 128:(j + 1) * 128, :] = lk[:, j * 128:(j + 1) * 128].T
    offset = (lax.broadcasted_iota(jnp.int32, (blk, win), 1)
              - lax.broadcasted_iota(jnp.int32, (blk, win), 0) - (PAD - BAND))

    def band_block(j, carry):
        start = pl.multiple_of(j * blk, 16)
        columns = lkt[pl.ds(start, blk), :]
        degree = start + lax.broadcasted_iota(jnp.int32, (blk, 128), 0)
        columns = jnp.where(degree >= me, columns, 0.0)
        for d in range(3):
            band = jnp.zeros((blk, win), F32)
            for k in range(2 * BAND + 1):
                band = jnp.where(offset == k, columns[:, 16 * d + k:16 * d + k + 1], band)
            high, low = split(band)
            bands[j, d, 0] = high
            bands[j, d, 1] = low
        return carry

    lax.fori_loop(0, nblk, band_block, 0)
    for d in range(3):
        coef[d, 0:PAD, :] = jnp.zeros((PAD, half), BF16)
        coef[d, PAD + degrees:, :] = jnp.zeros((PAD, half), BF16)

    @pl.when(me == 0)
    def _():
        coef[0] = jnp.zeros(coef.shape[1:], BF16)

    @pl.when(me == n - 1)
    def _():
        coef[2] = jnp.zeros(coef.shape[1:], BF16)

    loads[1].wait()
    loads[3].wait()
    away = pl.ds(0, (n - 1) * rows)
    for c in range(nchunk):
        pltpu.make_async_copy(recv.at[c, away, :], recv.at[c, away, :], a_recv.at[c]).wait()

    edges = [0] + [blk * (j + 1) + PAD for j in range(nblk - 1)] + [degrees]

    def neighbour(j, side):
        span = pl.ds(PAD + edges[j], edges[j + 1] - edges[j])
        to = jnp.maximum(me - 1, 0) if side == 0 else jnp.minimum(me + 1, n - 1)
        return pltpu.make_async_remote_copy(
            src_ref=coef.at[1, span, :], dst_ref=coef.at[2 if side == 0 else 0, span, :],
            send_sem=c_send.at[side, j], recv_sem=c_recv.at[side, j],
            device_id=(to,), device_id_type=MESH,
        )

    for j in range(nblk):
        low, high = edges[j], edges[j + 1]
        total = jnp.zeros((high - low, half), F32)
        for c in range(nchunk):
            total += lax.dot_general(
                leg[low:high, c * lat:(c + 1) * lat], recv[c],
                (((1,), (1,)), ((), ())), preferred_element_type=F32)
        degree = low + lax.broadcasted_iota(jnp.int32, (high - low, half), 0)
        coef[1, PAD + low:PAD + high, :] = jnp.where(degree >= me, total, 0.0).astype(BF16)

        @pl.when(me > 0)
        def _():
            neighbour(j, 0).start()

        @pl.when(me < n - 1)
        def _():
            neighbour(j, 1).start()

    def banded(j, d):
        window = coef[d, j * blk:j * blk + win, :]
        return (jnp.dot(bands[j, d, 0], window, preferred_element_type=F32)
                + jnp.dot(bands[j, d, 1], window, preferred_element_type=F32))

    for j in range(nblk):
        comb[j * blk:(j + 1) * blk, :] = banded(j, 1)

    def out_copy(j):
        span = pl.ds(j * blk, blk)
        return pltpu.make_async_copy(comb.at[span, :], out.at[0, span, :], out_sem.at[j])

    for j in range(nblk):
        @pl.when(me < n - 1)
        def _():
            neighbour(j, 0).wait_recv()

        @pl.when(me > 0)
        def _():
            neighbour(j, 1).wait_recv()

        high, low = split(comb[j * blk:(j + 1) * blk, :] + banded(j, 0) + banded(j, 2))
        comb[j * blk:(j + 1) * blk, :] = (
            jnp.dot(high, wt[...], preferred_element_type=F32)
            + jnp.dot(low, wt[...], preferred_element_type=F32))
        out_copy(j).start()

    for c in range(nchunk):
        pltpu.make_async_copy(send.at[c, away, :], send.at[c, away, :], a_send.at[c]).wait()
    for j in range(nblk):
        @pl.when(me > 0)
        def _():
            neighbour(j, 0).wait_send()

        @pl.when(me < n - 1)
        def _():
            neighbour(j, 1).wait_send()

        out_copy(j).wait()


def on_device(n, images, legendre, leakage):
    t_local, nlat, nlon = images.shape
    degrees = legendre.shape[1]
    ntimes = t_local * n
    half = 2 * ntimes
    lat = 256 if nlat % 256 == 0 else 128
    nchunk = nlat // lat
    nblk = 4 if half <= 1024 else degrees // 64
    blk = degrees // nblk
    table = jnp.asarray(lon_table(nlon, n))
    wtable = jnp.asarray(time_table(ntimes, n))
    wide = -(-degrees // 128) * 128
    anywhere = pl.BlockSpec(memory_space=pl.ANY)
    return pl.pallas_call(
        functools.partial(kernel, n, lat, nblk),
        out_shape=jax.ShapeDtypeStruct((1, degrees, half), F32),
        in_specs=[anywhere] * 5,
        out_specs=anywhere,
        scratch_shapes=[
            pltpu.VMEM(images.shape, BF16),
            pltpu.VMEM(table.shape, BF16),
            pltpu.VMEM(legendre.shape[1:], BF16),
            pltpu.VMEM(leakage.shape[1:], F32),
            pltpu.VMEM(wtable.shape, BF16),
            pltpu.VMEM((lat // 128, 2 * n * t_local, 128), F32),
            pltpu.VMEM((nchunk, half, lat), BF16),
            pltpu.VMEM((nchunk, half, lat), BF16),
            pltpu.VMEM((3, degrees + 2 * PAD, half), BF16),
            pltpu.VMEM((degrees, half), F32),
            pltpu.VMEM((nblk, 3, 2, blk, blk + 2 * PAD), BF16),
            pltpu.VMEM((128, wide), F32),
            pltpu.VMEM((wide, 128), F32),
            pltpu.SemaphoreType.DMA((nchunk, t_local)),
            pltpu.SemaphoreType.DMA((4,)),
            pltpu.SemaphoreType.DMA((nchunk,)),
            pltpu.SemaphoreType.DMA((nchunk,)),
            pltpu.SemaphoreType.DMA((2, nblk)),
            pltpu.SemaphoreType.DMA((2, nblk)),
            pltpu.SemaphoreType.DMA((nblk,)),
        ],
        compiler_params=pltpu.CompilerParams(
            collective_id=0, has_side_effects=True, vmem_limit_bytes=66_000_000),
    )(images, legendre, leakage, table, wtable)


def solution(mesh):
    placed = (P("dev", None, None), P("dev", None, None), P("dev", None, None, None))
    return jax.shard_map(
        functools.partial(on_device, mesh.shape["dev"]),
        mesh=mesh, in_specs=placed, out_specs=P("dev", None, None), check_vma=False,
    )
```

```python
import functools
import math

import jax
import jax.numpy as jnp
import numpy as np
from jax import lax
from jax.experimental import pallas as pl
from jax.experimental.pallas import tpu as pltpu
from jax.sharding import PartitionSpec as P

MESH = pl.DeviceIdType.MESH
BAND = 6
PAD = 16
F32 = jnp.float32
BF16 = jnp.bfloat16


def lon_table(nlon, norders):
    phase = (np.arange(nlon)[None, :] * np.arange(norders)[:, None]) % nlon
    angle = 2.0 * math.pi * phase / nlon
    table = np.stack([np.cos(angle), -np.sin(angle)], axis=1) / math.sqrt(nlon)
    return table.reshape(2 * norders, nlon).astype(np.float32).astype(BF16)


def time_table(ntimes, devices):
    phase = (np.arange(ntimes)[:, None] * np.arange(ntimes)[None, :]) % ntimes
    angle = 2.0 * math.pi * phase / ntimes
    cosine, sine = np.cos(angle), np.sin(angle)
    upper = np.concatenate([cosine, -sine], axis=1)
    lower = np.concatenate([sine, cosine], axis=1)
    table = np.concatenate([upper, lower], axis=0) / math.sqrt(ntimes)
    table = table.reshape(2, devices, ntimes // devices, 2 * ntimes).transpose(1, 0, 2, 3)
    return table.reshape(2 * ntimes, 2 * ntimes).astype(np.float32).astype(BF16)


def split(value):
    high = value.astype(BF16)
    low = (value - high.astype(F32)).astype(BF16)
    return high, low


def kernel(n, lat, nblk, ngrp,
           images, legendre, leakage, table, wtable, out,
           img, tab, leg, leak, wt, scr, send, recv, coef, acc, bands, lk, lkt,
           img_sem, in_sem, a_send, a_recv, c_send, c_recv, out_sem):
    me = lax.axis_index("dev")
    t_local, nlat, nlon = images.shape
    rows = 2 * t_local
    nchunk = nlat // lat
    ktab = 2 * n
    grp = n // ngrp
    wide = grp * rows
    group, place = me // grp, lax.rem(me, grp)
    degrees = legendre.shape[1]
    blk = degrees // nblk
    win = blk + 2 * PAD
    half = wtable.shape[0]

    def load(index, src, dst):
        return pltpu.make_async_copy(src, dst, in_sem.at[index])

    def image_copy(c, t):
        part = pl.ds(c * lat, lat)
        return pltpu.make_async_copy(images.at[t, part, :], img.at[t, part, :], img_sem.at[c, t])

    loads = [
        load(0, table, tab), load(1, legendre.at[0], leg), load(2, leakage, leak),
        load(3, wtable, wt),
    ]
    loads[0].start()
    for c in range(nchunk):
        for t in range(t_local):
            image_copy(c, t).start()
    for copy in loads[1:]:
        copy.start()

    barrier = pltpu.get_barrier_semaphore()

    def greet(o, carry):
        pl.semaphore_signal(barrier, inc=1, device_id=(lax.rem(me + o, n),), device_id_type=MESH)
        return carry

    lax.fori_loop(1, n, greet, 0)
    loads[0].wait()

    def lon_chunk(c, carry):
        for t in range(t_local):
            image_copy(c, t).wait()
        block = img[:, pl.ds(pl.multiple_of(c * lat, lat), lat), :].reshape(t_local * lat, nlon)
        whole = jnp.dot(block, tab[...], preferred_element_type=F32)
        for t in range(t_local):
            part = whole[t * lat:(t + 1) * lat].T[:ktab]
            for j in range(lat // 128):
                scr[j, pl.ds(t, ktab, stride=t_local), :] = part[:, j * 128:(j + 1) * 128]
        for j in range(lat // 128):
            send[c, :, j * 128:(j + 1) * 128] = scr[j].astype(BF16)

        @pl.when(c == 0)
        def _():
            pl.semaphore_wait(barrier, n - 1)

        mine = pl.ds(pl.multiple_of(me * rows, rows), rows)

        def post(o, inner):
            step, seat = o // grp, lax.rem(o, grp)
            to = lax.rem(group + step, ngrp) * grp + lax.rem(place + seat, grp)
            theirs = pl.ds(pl.multiple_of(to * rows, rows), rows)
            pltpu.make_async_remote_copy(
                src_ref=send.at[c, theirs, :], dst_ref=recv.at[c, mine, :],
                send_sem=a_send.at[c], recv_sem=a_recv.at[step, c],
                device_id=(to,), device_id_type=MESH,
            ).start()
            return inner

        lax.fori_loop(1, n, post, 0)
        recv[c, mine, :] = send[c, mine, :]
        return carry

    lax.fori_loop(0, nchunk, lon_chunk, 0)

    loads[2].wait()
    lk[...] = jnp.zeros_like(lk)
    for d in range(3):
        for k in range(2 * BAND + 1):
            lk[16 * d + k:16 * d + k + 1, 0:degrees] = leak[k, d]
    for j in range(lk.shape[1] // 128):
        lkt[j * 128:(j + 1) * 128, :] = lk[:, j * 128:(j + 1) * 128].T
    offset = (lax.broadcasted_iota(jnp.int32, (blk, win), 1)
              - lax.broadcasted_iota(jnp.int32, (blk, win), 0) - (PAD - BAND))

    def band_block(j, carry):
        start = pl.multiple_of(j * blk, 16)
        columns = lkt[pl.ds(start, blk), :]
        degree = start + lax.broadcasted_iota(jnp.int32, (blk, 128), 0)
        columns = jnp.where(degree >= me, columns, 0.0)
        for d in range(3):
            band = jnp.zeros((blk, win), F32)
            for k in range(2 * BAND + 1):
                band = jnp.where(offset == k, columns[:, 16 * d + k:16 * d + k + 1], band)
            high, low = split(band)
            bands[j, d, 0:blk, :] = high
            bands[j, d, blk:, :] = low
        return carry

    lax.fori_loop(0, nblk, band_block, 0)
    margin = jnp.zeros((PAD, wide), BF16)
    for d in range(3):
        for g in range(ngrp):
            coef[d, g, 0:PAD, :] = margin
            coef[d, g, PAD + degrees:, :] = margin
    acc[...] = jnp.zeros_like(acc)
    loads[1].wait()
    loads[3].wait()

    def accumulate(d, g):
        rows_of = pl.ds(pl.multiple_of(g * wide, wide), wide)
        for j in range(nblk):
            span = slice(j * blk, (j + 1) * blk)
            both = jnp.dot(bands[j, d], coef[d, g, j * blk:j * blk + win, :], preferred_element_type=F32)
            high, low = split(both[:blk] + both[blk:])
            acc[span, :] += (jnp.dot(high, wt[rows_of, :], preferred_element_type=F32)
                             + jnp.dot(low, wt[rows_of, :], preferred_element_type=F32))

    def neighbour(i, g, side):
        span = pl.ds(PAD, degrees)
        to = jnp.maximum(me - 1, 0) if side == 0 else jnp.minimum(me + 1, n - 1)
        return pltpu.make_async_remote_copy(
            src_ref=coef.at[1, g, span, :], dst_ref=coef.at[2 if side == 0 else 0, g, span, :],
            send_sem=c_send.at[side, i], recv_sem=c_recv.at[side, i],
            device_id=(to,), device_id_type=MESH,
        )

    def nth(i, device):
        return lax.rem(device // grp - i + ngrp, ngrp)

    def coef_group(i, carry):
        for c in range(nchunk):
            @pl.when(i == 0)
            def _():
                piece = recv.at[c, pl.ds(0, (grp - 1) * rows), :]
                pltpu.make_async_copy(piece, piece, a_recv.at[0, c]).wait()

            @pl.when(i > 0)
            def _():
                piece = recv.at[c, pl.ds(0, wide), :]
                pltpu.make_async_copy(piece, piece, a_recv.at[i, c]).wait()

        g = nth(i, me)
        rows_of = pl.ds(pl.multiple_of(g * wide, wide), wide)
        total = jnp.zeros((degrees, wide), F32)
        for c in range(nchunk):
            total += lax.dot_general(
                leg[:, c * lat:(c + 1) * lat], recv[c, rows_of, :],
                (((1,), (1,)), ((), ())), preferred_element_type=F32)
        degree = lax.broadcasted_iota(jnp.int32, (degrees, wide), 0)
        coef[1, g, PAD:PAD + degrees, :] = jnp.where(degree >= me, total, 0.0).astype(BF16)

        @pl.when(me > 0)
        def _():
            neighbour(i, g, 0).start()

        @pl.when(me < n - 1)
        def _():
            neighbour(i, g, 1).start()

        accumulate(1, g)
        return carry

    lax.fori_loop(0, ngrp, coef_group, 0)

    def side_group(i, carry):
        @pl.when(me < n - 1)
        def _():
            g = nth(i, me + 1)
            neighbour(i, g, 0).wait_recv()
            accumulate(2, g)

        @pl.when(me > 0)
        def _():
            g = nth(i, me - 1)
            neighbour(i, g, 1).wait_recv()
            accumulate(0, g)

        return carry

    lax.fori_loop(0, ngrp, side_group, 0)
    result = pltpu.make_async_copy(acc, out.at[0], out_sem)
    result.start()

    away = pl.ds(0, (n - 1) * rows)
    for c in range(nchunk):
        pltpu.make_async_copy(send.at[c, away, :], send.at[c, away, :], a_send.at[c]).wait()

    def sent(i, carry):
        g = nth(i, me)

        @pl.when(me > 0)
        def _():
            neighbour(i, g, 0).wait_send()

        @pl.when(me < n - 1)
        def _():
            neighbour(i, g, 1).wait_send()

        return carry

    lax.fori_loop(0, ngrp, sent, 0)
    result.wait()


def on_device(n, images, legendre, leakage):
    t_local, nlat, nlon = images.shape
    degrees = legendre.shape[1]
    ntimes = t_local * n
    half = 2 * ntimes
    lat = 256 if nlat % 256 == 0 else 128
    nchunk = nlat // lat
    nblk = 4 if half <= 1024 else degrees // 64
    blk = degrees // nblk
    ngrp = half // 128
    table = lon_table(nlon, n).T
    table = jnp.asarray(np.concatenate([table, np.zeros((nlon, -2 * n % 128), BF16)], axis=1))
    leakage = leakage.transpose(2, 1, 0, 3)
    wtable = jnp.asarray(time_table(ntimes, n))
    wide = -(-degrees // 128) * 128
    anywhere = pl.BlockSpec(memory_space=pl.ANY)
    return pl.pallas_call(
        functools.partial(kernel, n, lat, nblk, ngrp),
        out_shape=jax.ShapeDtypeStruct((1, degrees, half), F32),
        in_specs=[anywhere] * 5,
        out_specs=anywhere,
        scratch_shapes=[
            pltpu.VMEM(images.shape, BF16),
            pltpu.VMEM(table.shape, BF16),
            pltpu.VMEM(legendre.shape[1:], BF16),
            pltpu.VMEM(leakage.shape, F32),
            pltpu.VMEM(wtable.shape, BF16),
            pltpu.VMEM((lat // 128, 2 * n * t_local, 128), F32),
            pltpu.VMEM((nchunk, half, lat), BF16),
            pltpu.VMEM((nchunk, half, lat), BF16),
            pltpu.VMEM((3, ngrp, degrees + 2 * PAD, half // ngrp), BF16),
            pltpu.VMEM((degrees, half), F32),
            pltpu.VMEM((nblk, 3, 2 * blk, blk + 2 * PAD), BF16),
            pltpu.VMEM((128, wide), F32),
            pltpu.VMEM((wide, 128), F32),
            pltpu.SemaphoreType.DMA((nchunk, t_local)),
            pltpu.SemaphoreType.DMA((4,)),
            pltpu.SemaphoreType.DMA((nchunk,)),
            pltpu.SemaphoreType.DMA((ngrp, nchunk)),
            pltpu.SemaphoreType.DMA((2, ngrp)),
            pltpu.SemaphoreType.DMA((2, ngrp)),
            pltpu.SemaphoreType.DMA,
        ],
        compiler_params=pltpu.CompilerParams(
            collective_id=0, has_side_effects=True, vmem_limit_bytes=66_000_000),
    )(images, legendre, leakage, table, wtable)


def solution(mesh):
    placed = (P("dev", None, None), P("dev", None, None), P("dev", None, None, None))
    return jax.shard_map(
        functools.partial(on_device, mesh.shape["dev"]),
        mesh=mesh, in_specs=placed, out_specs=P("dev", None, None), check_vma=False,
    )
```

```python
import functools
import math

import jax
import jax.numpy as jnp
import numpy as np
from jax import lax
from jax.experimental import pallas as pl
from jax.experimental.pallas import tpu as pltpu
from jax.sharding import PartitionSpec as P

MESH = pl.DeviceIdType.MESH
BAND = 6
PAD = 16
F32 = jnp.float32
BF16 = jnp.bfloat16


def lon_table(nlon, norders):
    phase = (np.arange(nlon)[None, :] * np.arange(norders)[:, None]) % nlon
    angle = 2.0 * math.pi * phase / nlon
    table = np.stack([np.cos(angle), -np.sin(angle)], axis=1) / math.sqrt(nlon)
    return table.reshape(2 * norders, nlon).astype(np.float32).astype(BF16)


def time_table(ntimes, devices):
    phase = (np.arange(ntimes)[:, None] * np.arange(ntimes)[None, :]) % ntimes
    angle = 2.0 * math.pi * phase / ntimes
    cosine, sine = np.cos(angle), np.sin(angle)
    upper = np.concatenate([cosine, -sine], axis=1)
    lower = np.concatenate([sine, cosine], axis=1)
    table = np.concatenate([upper, lower], axis=0) / math.sqrt(ntimes)
    table = table.reshape(2, devices, ntimes // devices, 2 * ntimes).transpose(1, 0, 2, 3)
    return table.reshape(2 * ntimes, 2 * ntimes).astype(np.float32).astype(BF16)


def split(value):
    high = value.astype(BF16)
    low = (value - high.astype(F32)).astype(BF16)
    return high, low


def kernel(n, lat, nblk, ngrp,
           images, legendre, leakage, table, wtable, out,
           img, tab, leg, leak, wt, scr, send, recv, coef, acc, bands, lk, lkt,
           img_sem, in_sem, a_send, a_recv, c_send, c_recv, out_sem):
    me = lax.axis_index("dev")
    t_local, nlat, nlon = images.shape
    rows = 2 * t_local
    nchunk = nlat // lat
    ktab = 2 * n
    grp = n // ngrp
    wide = grp * rows
    group, place = me // grp, lax.rem(me, grp)
    degrees = legendre.shape[1]
    blk = degrees // nblk
    win = blk + 2 * PAD
    half = wtable.shape[0]

    def load(index, src, dst):
        return pltpu.make_async_copy(src, dst, in_sem.at[index])

    def image_copy(c, t):
        part = pl.ds(c * lat, lat)
        return pltpu.make_async_copy(images.at[t, part, :], img.at[t, part, :], img_sem.at[c, t])

    loads = [
        load(0, table, tab), load(1, legendre.at[0], leg), load(2, leakage, leak),
        load(3, wtable, wt),
    ]
    loads[0].start()
    for c in range(nchunk):
        for t in range(t_local):
            image_copy(c, t).start()
    for copy in loads[1:]:
        copy.start()

    barrier = pltpu.get_barrier_semaphore()

    def greet(o, carry):
        pl.semaphore_signal(barrier, inc=1, device_id=(lax.rem(me + o, n),), device_id_type=MESH)
        return carry

    lax.fori_loop(1, n, greet, 0)
    loads[0].wait()

    def lon_chunk(c, carry):
        for t in range(t_local):
            image_copy(c, t).wait()
        block = img[:, pl.ds(pl.multiple_of(c * lat, lat), lat), :].reshape(t_local * lat, nlon)
        whole = jnp.dot(block, tab[...], preferred_element_type=F32)
        for t in range(t_local):
            part = whole[t * lat:(t + 1) * lat].T[:ktab]
            for j in range(lat // 128):
                scr[j, pl.ds(t, ktab, stride=t_local), :] = part[:, j * 128:(j + 1) * 128]
        for j in range(lat // 128):
            send[c, :, j * 128:(j + 1) * 128] = scr[j].astype(BF16)

        @pl.when(c == 0)
        def _():
            pl.semaphore_wait(barrier, n - 1)

        mine = pl.ds(pl.multiple_of(me * rows, rows), rows)

        def post(o, inner):
            step, seat = o // grp, lax.rem(o, grp)
            to = lax.rem(group + step, ngrp) * grp + lax.rem(place + seat, grp)
            theirs = pl.ds(pl.multiple_of(to * rows, rows), rows)
            pltpu.make_async_remote_copy(
                src_ref=send.at[c, theirs, :], dst_ref=recv.at[c, mine, :],
                send_sem=a_send.at[c], recv_sem=a_recv.at[step, c],
                device_id=(to,), device_id_type=MESH,
            ).start()
            return inner

        lax.fori_loop(1, n, post, 0)
        recv[c, mine, :] = send[c, mine, :]
        return carry

    lax.fori_loop(0, nchunk, lon_chunk, 0)

    loads[2].wait()
    lk[...] = jnp.zeros_like(lk)
    for d in range(3):
        for k in range(2 * BAND + 1):
            lk[16 * d + k:16 * d + k + 1, 0:degrees] = leak[d, k]
    for j in range(lk.shape[1] // 128):
        lkt[j * 128:(j + 1) * 128, :] = lk[:, j * 128:(j + 1) * 128].T
    offset = (lax.broadcasted_iota(jnp.int32, (blk, win), 1)
              - lax.broadcasted_iota(jnp.int32, (blk, win), 0) - (PAD - BAND))

    def band_block(j, carry):
        start = pl.multiple_of(j * blk, 16)
        columns = lkt[pl.ds(start, blk), :]
        degree = start + lax.broadcasted_iota(jnp.int32, (blk, 128), 0)
        columns = jnp.where(degree >= me, columns, 0.0)
        for d in range(3):
            band = jnp.zeros((blk, win), F32)
            for k in range(2 * BAND + 1):
                band = jnp.where(offset == k, columns[:, 16 * d + k:16 * d + k + 1], band)
            high, low = split(band)
            bands[j, d, 0:blk, :] = high
            bands[j, d, blk:, :] = low
        return carry

    lax.fori_loop(0, nblk, band_block, 0)
    margin = jnp.zeros((PAD, wide), BF16)
    for d in range(3):
        for g in range(ngrp):
            coef[d, g, 0:PAD, :] = margin
            coef[d, g, PAD + degrees:, :] = margin
    loads[1].wait()
    loads[3].wait()

    def accumulate(d, g):
        columns_of = pl.ds(pl.multiple_of(g * wide, wide), wide)
        for j in range(nblk):
            span = slice(j * blk, (j + 1) * blk)
            both = jnp.dot(bands[j, d], coef[d, g, j * blk:j * blk + win, :], preferred_element_type=F32)
            both = both[:blk] + both[blk:]
            if d == 1:
                acc[span, columns_of] = both
            else:
                acc[span, columns_of] += both

    def neighbour(i, g, side):
        span = pl.ds(PAD, degrees)
        to = jnp.maximum(me - 1, 0) if side == 0 else jnp.minimum(me + 1, n - 1)
        return pltpu.make_async_remote_copy(
            src_ref=coef.at[1, g, span, :], dst_ref=coef.at[2 if side == 0 else 0, g, span, :],
            send_sem=c_send.at[side, i], recv_sem=c_recv.at[side, i],
            device_id=(to,), device_id_type=MESH,
        )

    def nth(i, device):
        return lax.rem(device // grp - i + ngrp, ngrp)

    def coef_group(i, carry):
        for c in range(nchunk):
            @pl.when(i == 0)
            def _():
                piece = recv.at[c, pl.ds(0, (grp - 1) * rows), :]
                pltpu.make_async_copy(piece, piece, a_recv.at[0, c]).wait()

            @pl.when(i > 0)
            def _():
                piece = recv.at[c, pl.ds(0, wide), :]
                pltpu.make_async_copy(piece, piece, a_recv.at[i, c]).wait()

        g = nth(i, me)
        rows_of = pl.ds(pl.multiple_of(g * wide, wide), wide)
        total = jnp.zeros((degrees, wide), F32)
        for c in range(nchunk):
            total += lax.dot_general(
                leg[:, c * lat:(c + 1) * lat], recv[c, rows_of, :],
                (((1,), (1,)), ((), ())), preferred_element_type=F32)
        degree = lax.broadcasted_iota(jnp.int32, (degrees, wide), 0)
        coef[1, g, PAD:PAD + degrees, :] = jnp.where(degree >= me, total, 0.0).astype(BF16)

        @pl.when(me > 0)
        def _():
            neighbour(i, g, 0).start()

        @pl.when(me < n - 1)
        def _():
            neighbour(i, g, 1).start()

        accumulate(1, g)
        return carry

    lax.fori_loop(0, ngrp, coef_group, 0)

    def side_group(i, carry):
        @pl.when(me < n - 1)
        def _():
            g = nth(i, me + 1)
            neighbour(i, g, 0).wait_recv()
            accumulate(2, g)

        @pl.when(me > 0)
        def _():
            g = nth(i, me - 1)
            neighbour(i, g, 1).wait_recv()
            accumulate(0, g)

        return carry

    lax.fori_loop(0, ngrp, side_group, 0)

    def out_copy(j):
        span = pl.ds(j * blk, blk)
        return pltpu.make_async_copy(acc.at[span, :], out.at[0, span, :], out_sem.at[j])

    depth = min(half, 512)
    for j in range(nblk):
        span = slice(j * blk, (j + 1) * blk)
        high, low = split(acc[span, :])
        total = jnp.zeros((blk, half), F32)
        for k in range(0, half, depth):
            total += (jnp.dot(high[:, k:k + depth], wt[k:k + depth, :], preferred_element_type=F32)
                      + jnp.dot(low[:, k:k + depth], wt[k:k + depth, :], preferred_element_type=F32))
        acc[span, :] = total
        out_copy(j).start()

    away = pl.ds(0, (n - 1) * rows)
    for c in range(nchunk):
        pltpu.make_async_copy(send.at[c, away, :], send.at[c, away, :], a_send.at[c]).wait()

    def sent(i, carry):
        g = nth(i, me)

        @pl.when(me > 0)
        def _():
            neighbour(i, g, 0).wait_send()

        @pl.when(me < n - 1)
        def _():
            neighbour(i, g, 1).wait_send()

        return carry

    lax.fori_loop(0, ngrp, sent, 0)
    for j in range(nblk):
        out_copy(j).wait()


def on_device(n, images, legendre, leakage):
    t_local, nlat, nlon = images.shape
    degrees = legendre.shape[1]
    ntimes = t_local * n
    half = 2 * ntimes
    lat = 256 if nlat % 256 == 0 else 128
    nchunk = nlat // lat
    nblk = 4 if half <= 1024 else degrees // 64
    blk = degrees // nblk
    ngrp = half // 128
    table = lon_table(nlon, n).T
    table = jnp.asarray(np.concatenate([table, np.zeros((nlon, -2 * n % 128), BF16)], axis=1))
    leakage = leakage.transpose(1, 2, 0, 3)
    wtable = jnp.asarray(time_table(ntimes, n))
    wide = -(-degrees // 128) * 128
    anywhere = pl.BlockSpec(memory_space=pl.ANY)
    return pl.pallas_call(
        functools.partial(kernel, n, lat, nblk, ngrp),
        out_shape=jax.ShapeDtypeStruct((1, degrees, half), F32),
        in_specs=[anywhere] * 5,
        out_specs=anywhere,
        scratch_shapes=[
            pltpu.VMEM(images.shape, BF16),
            pltpu.VMEM(table.shape, BF16),
            pltpu.VMEM(legendre.shape[1:], BF16),
            pltpu.VMEM(leakage.shape, F32),
            pltpu.VMEM(wtable.shape, BF16),
            pltpu.VMEM((lat // 128, 2 * n * t_local, 128), F32),
            pltpu.VMEM((nchunk, half, lat), BF16),
            pltpu.VMEM((nchunk, half, lat), BF16),
            pltpu.VMEM((3, ngrp, degrees + 2 * PAD, half // ngrp), BF16),
            pltpu.VMEM((degrees, half), F32),
            pltpu.VMEM((nblk, 3, 2 * blk, blk + 2 * PAD), BF16),
            pltpu.VMEM((128, wide), F32),
            pltpu.VMEM((wide, 128), F32),
            pltpu.SemaphoreType.DMA((nchunk, t_local)),
            pltpu.SemaphoreType.DMA((4,)),
            pltpu.SemaphoreType.DMA((nchunk,)),
            pltpu.SemaphoreType.DMA((ngrp, nchunk)),
            pltpu.SemaphoreType.DMA((2, ngrp)),
            pltpu.SemaphoreType.DMA((2, ngrp)),
            pltpu.SemaphoreType.DMA((nblk,)),
        ],
        compiler_params=pltpu.CompilerParams(
            collective_id=0, has_side_effects=True, vmem_limit_bytes=66_000_000),
    )(images, legendre, leakage, table, wtable)


def solution(mesh):
    placed = (P("dev", None, None), P("dev", None, None), P("dev", None, None, None))
    return jax.shard_map(
        functools.partial(on_device, mesh.shape["dev"]),
        mesh=mesh, in_specs=placed, out_specs=P("dev", None, None), check_vma=False,
    )
```
